32 devices in a mesh: slab: 4 (over y, x), brick: 8 (over z, core).
Axes of the slice: x: 2, y: 2, z: 4, core: 2. Of those that a mesh axis runs over, the one named last changes fastest.
Arguments:
- k_coeffs: float32 [8, 16, 16, 128], P('slab', 'brick'), may hold values from -0.3 to 0.4
- v_basis: float32 [32768, 128], P(('slab', 'brick')), may hold values from -4 to 4
Outputs:
- basis_x: float32 [8, 16, 16, 128], P('slab', 'brick')
- coupling: float32 [128, 128], replicated
- basis_v: float32 [32768, 128], P(('slab', 'brick'))
The draws below stay inside these ranges and needn't reach their ends.
All inputs are finite; a program needn't handle non-finite values.
Results may differ from the reference program's by a relative error of at most 0.0001.
Values sent between devices are 32-bit elements; how exact they have to be, the bound alone decides.
A program may use at most 64 MiB of HBM per device.

```python
import math
import jax
import jax.numpy as jnp
from jax import lax

R = 128
NVX = 32
NV = 32768
NZ = 16
NX = 8
NY = 16


VMAX = 6.0


def node_velocities(indices):
    spacing = 2.0 * VMAX / NVX
    first_index = indices // (NVX * NVX)
    second = indices // NVX % NVX
    third_index = indices % NVX
    coords = jnp.stack([first_index, second, third_index]).astype(jnp.float32)
    return -VMAX + (coords + 0.5) * spacing


def draw_v_basis(key, part):
    velocity = node_velocities(jnp.arange(NV, dtype=jnp.int32))
    square = jnp.sum(velocity * velocity, axis=0)
    gaussian = jnp.exp(-0.5 * square)
    smooth = jnp.stack([gaussian, velocity[0] * gaussian, velocity[1] * gaussian, velocity[2] * gaussian, (square - 3.0) * gaussian], axis=1)
    rough_part = jnp.clip(jax.random.normal(key, (NV, R - 5), jnp.float32), -4.0, 4.0) * jnp.exp(-0.25 * square)[:, None]
    columns = jnp.concatenate([smooth, rough_part], axis=1)
    weight_v = (2.0 * VMAX / NVX) ** 3
    identity = jnp.eye(R, dtype=jnp.float32)
    for sweep_index in range(2):
        gram_matrix = lax.dot_general(columns, columns, (((0,), (0,)), ((), ())), precision=lax.Precision.HIGHEST) * weight_v
        factor = jnp.linalg.cholesky(gram_matrix)
        inverse = jax.scipy.linalg.solve_triangular(factor, identity, lower=True)
        columns = jnp.dot(columns, inverse.T, precision=lax.Precision.HIGHEST)
    return columns.astype(jnp.float32)


def draw_k_coeffs(key, part):
    subkeys = jax.random.split(key, 3)
    rough_part = jnp.clip(jax.random.normal(subkeys[0], (NX, NY, NZ, R), jnp.float32), -5.0, 5.0) * 0.05
    density = jnp.exp(jax.random.uniform(subkeys[1], (NX, NY, NZ), jnp.float32, math.log(0.03), math.log(0.3)))
    row_scale = jnp.concatenate([jnp.zeros((1,), jnp.float32), jnp.full((4,), 0.6, jnp.float32), jnp.ones((R - 5,), jnp.float32)])
    return (rough_part * row_scale).at[..., 0].set(density).astype(jnp.float32)


def setup_inputs(seed: int = 0) -> dict:
    arg_keys = jax.random.split(jax.random.key(seed), 3)
    return {
        "k_coeffs": draw_k_coeffs(jax.random.fold_in(arg_keys[2], 71), 0),
        "v_basis": draw_v_basis(jax.random.fold_in(arg_keys[2], 71), 0),
    }


CFL = 0.9
VMAX = 6.0
COLLIDE = 0.3
RHO_MIN = 0.25
TEMP_MIN = 0.25
PRECISE = lax.Precision.HIGHEST

def velocities(indices):
    spacing = 2.0 * VMAX / NVX
    first_index = indices // (NVX * NVX)
    second = indices // NVX % NVX
    third_index = indices % NVX
    coords = jnp.stack([first_index, second, third_index]).astype(jnp.float32)
    return -VMAX + (coords + 0.5) * spacing

def maxwell(cell_params, velocity):
    distance = (velocity[0][None, :] - cell_params[1][:, None]) ** 2
    distance = distance + (velocity[1][None, :] - cell_params[2][:, None]) ** 2
    distance = distance + (velocity[2][None, :] - cell_params[3][:, None]) ** 2
    amplitude = cell_params[0] * (2.0 * math.pi * cell_params[4]) ** (-1.5)
    return amplitude[:, None] * jnp.exp(distance * (-0.5 / cell_params[4])[:, None])

def cell_state(vectors, coeffs):
    moments = lax.dot_general(vectors, coeffs, (((1,), (1,)), ((), ())), precision=PRECISE)
    density = jnp.maximum(moments[0], RHO_MIN)
    drift_speed = moments[1:4] / density[None, :]
    temper = jnp.maximum((moments[4] / density - jnp.sum(drift_speed * drift_speed, axis=0)) / 3.0, TEMP_MIN)
    return jnp.concatenate([density[None], drift_speed, temper[None]], axis=0)

def transport_flux(backward, forward, transport):
    flux = jnp.zeros_like(backward[0])
    for axis_id in range(3):
        flux = flux + jnp.dot(backward[axis_id], transport[axis_id], precision=PRECISE)
        flux = flux + jnp.dot(forward[axis_id], transport[3 + axis_id], precision=PRECISE)
    return flux

def products(left_side, backward, forward, maxwell_proj):
    pieces = [lax.dot_general(left_side, item, (((0,), (0,)), ((), ())), precision=PRECISE) for item in backward + forward + [maxwell_proj]]
    return jnp.stack(pieces)

def coupling_step(coupling_hat, minus_side, plus_side, projected, transport, time_step):
    drift_sum = jnp.zeros_like(coupling_hat)
    for axis_id in range(3):
        drift_sum = drift_sum + jnp.dot(jnp.dot(minus_side[axis_id], coupling_hat, precision=PRECISE), transport[axis_id], precision=PRECISE)
        drift_sum = drift_sum + jnp.dot(jnp.dot(plus_side[axis_id], coupling_hat, precision=PRECISE), transport[3 + axis_id], precision=PRECISE)
    return coupling_hat + time_step * drift_sum - COLLIDE * (projected - coupling_hat)

def velocity_step(velocity_part, minus_side, plus_side, back_proj, positive, negative, time_step):
    drift_sum = jnp.zeros_like(velocity_part)
    for axis_id in range(3):
        drift_sum = drift_sum + positive[axis_id][:, None] * jnp.dot(velocity_part, minus_side[axis_id].T, precision=PRECISE)
        drift_sum = drift_sum + negative[axis_id][:, None] * jnp.dot(velocity_part, plus_side[axis_id].T, precision=PRECISE)
    return velocity_part - time_step * drift_sum + COLLIDE * (back_proj - velocity_part)

def slopes(field):
    rank_size = field.shape[3]
    lengths = (NX, NY, NZ)
    backward = [((field - jnp.roll(field, 1, axis=axis_id)) * lengths[axis_id]).reshape(-1, rank_size) for axis_id in range(3)]
    forward = [((jnp.roll(field, -1, axis=axis_id) - field) * lengths[axis_id]).reshape(-1, rank_size) for axis_id in range(3)]
    return (backward, forward)

def reference(k_coeffs, v_basis):
    rank_size = k_coeffs.shape[3]
    cell_count = NX * NY * NZ
    time_step = CFL / (VMAX * (NX + NY + NZ))
    weight_x = 1.0 / cell_count
    weight_v = (2.0 * VMAX / NVX) ** 3
    velocity = velocities(jnp.arange(NV, dtype=jnp.int32))
    positive = jnp.maximum(velocity, 0.0)
    negative = jnp.minimum(velocity, 0.0)
    weights = jnp.stack([jnp.ones_like(velocity[0]), velocity[0], velocity[1], velocity[2], jnp.sum(velocity * velocity, axis=0)])
    vectors = jnp.dot(weights, v_basis, precision=PRECISE) * weight_v
    transport = jnp.stack([lax.dot_general(v_basis * (side[axis_id] * weight_v)[:, None], v_basis, (((0,), (0,)), ((), ())), precision=PRECISE) for side in (positive, negative) for axis_id in range(3)])
    coeff_flat = k_coeffs.reshape(cell_count, rank_size)
    cell_params = cell_state(vectors, coeff_flat)
    block_rows = math.gcd(NV, 2048)
    block_total = NV // block_rows
    vel_blocks = velocity.reshape(3, block_total, block_rows).transpose(1, 0, 2)
    basis_blocks = v_basis.reshape(block_total, block_rows, rank_size)

    def add_block(accumulated, pair):
        return (accumulated + jnp.dot(maxwell(cell_params, pair[0]), pair[1], precision=PRECISE) * weight_v, None)
    maxwell_proj = lax.scan(add_block, jnp.zeros((cell_count, rank_size), jnp.float32), (vel_blocks, basis_blocks))[0]
    backward, forward = slopes(k_coeffs)
    advanced = coeff_flat - time_step * transport_flux(backward, forward, transport) + COLLIDE * (maxwell_proj - coeff_flat)
    gram_matrix = lax.dot_general(advanced, advanced, (((0,), (0,)), ((), ())), precision=PRECISE) * weight_x
    factor = jnp.linalg.cholesky(gram_matrix)
    identity = jnp.eye(rank_size, dtype=jnp.float32)
    inverse = jax.scipy.linalg.solve_triangular(factor, identity, lower=True)
    basis_new = jnp.dot(advanced, inverse.T, precision=PRECISE)
    backward, forward = slopes(basis_new.reshape(NX, NY, NZ, rank_size))
    reduced = products(basis_new, backward, forward, maxwell_proj) * weight_x
    coupling_mid = coupling_step(factor.T, reduced[0:3], reduced[3:6], reduced[6], transport, time_step)

    def back_block(vblock):
        return lax.dot_general(maxwell(cell_params, vblock), basis_new, (((0,), (0,)), ((), ())), precision=PRECISE) * weight_x
    back_proj = lax.map(back_block, vel_blocks).reshape(NV, rank_size)
    velocity_part = jnp.dot(v_basis, coupling_mid.T, precision=PRECISE)
    velocity_new = velocity_step(velocity_part, reduced[0:3], reduced[3:6], back_proj, positive, negative, time_step)
    gram_v = lax.dot_general(velocity_new, velocity_new, (((0,), (0,)), ((), ())), precision=PRECISE) * weight_v
    coupling = jnp.linalg.cholesky(gram_v)
    inverse_v = jax.scipy.linalg.solve_triangular(coupling, identity, lower=True)
    vbasis_new = jnp.dot(velocity_new, inverse_v.T, precision=PRECISE)
    return (basis_new.reshape(NX, NY, NZ, rank_size), coupling, vbasis_new)
```

```python
import functools
import math

import jax
import jax.numpy as jnp
from jax import lax
from jax.experimental import pallas as pl
from jax.experimental.pallas import tpu as pltpu
from jax.sharding import PartitionSpec as P

NVX = 32

CFL = 0.9
VMAX = 6.0
COLLIDE = 0.3
RHO_MIN = 0.25
TEMP_MIN = 0.25
PRECISE = lax.Precision.HIGHEST
FAST = lax.Precision.HIGH
MESH = pl.DeviceIdType.MESH
VM = pl.BlockSpec(memory_space=pltpu.VMEM)


def dims():
    return 2, lax.axis_size("slab"), lax.axis_size("brick") // 2


def place():
    brick = lax.axis_index("brick")
    return lax.rem(brick, 2), lax.axis_index("slab"), lax.div(brick, 2)


def greet(sizes, me):
    _, slabs, layers = sizes
    core, slab, layer = me
    barrier = pltpu.get_barrier_semaphore()
    peers = [(slab, 2 * layer + 1 - core)]
    peers += [(lax.rem(slab + k, slabs), 2 * layer + core) for k in range(1, slabs)]
    peers += [(slab, 2 * lax.rem(layer + k, layers) + core) for k in range(1, layers)]
    for peer in peers:
        pl.semaphore_signal(barrier, inc=1, device_id=peer, device_id_type=MESH)
    pl.semaphore_wait(barrier, len(peers))


def spread(sizes, me, own, out, sems):
    _, slabs, layers = sizes
    core, slab, layer = me
    a_send, a_recv, b_send, b_recv, c_send, c_recv = sems
    partner = (slab, 2 * layer + 1 - core)
    started = []

    def send(source, target, send_sem, recv_sem, device):
        copy = pltpu.make_async_remote_copy(
            src_ref=source,
            dst_ref=target,
            send_sem=send_sem,
            recv_sem=recv_sem,
            device_id=device,
            device_id_type=MESH,
        )
        copy.start()
        started.append(copy)
        return copy

    def to_slabs(source, target, j):
        return [
            send(
                source,
                target,
                b_send.at[k - 1, j],
                b_recv.at[k - 1, j],
                (lax.rem(slab + k, slabs), 2 * layer + core),
            )
            for k in range(1, slabs)
        ]

    here = out.at[core, slab, layer]
    along = [
        send(own, here, a_send.at[k - 1], a_recv.at[k - 1], (slab, 2 * lax.rem(layer + k, layers) + core))
        for k in range(1, layers)
    ]
    crossing = [to_slabs(own, here, 0)]
    last = [send(own, here, c_send.at[0, 0], c_recv.at[0, 0], partner)]
    for j in range(1, layers):
        along[j - 1].wait_recv()
        block = out.at[core, slab, lax.rem(layer + layers - j, layers)]
        crossing.append(to_slabs(block, block, j))
        last.append(send(block, block, c_send.at[0, j], c_recv.at[0, j], partner))
    for j in range(layers):
        for k in range(1, slabs):
            crossing[j][k - 1].wait_recv()
            block = out.at[
                core, lax.rem(slab + slabs - k, slabs), lax.rem(layer + layers - j, layers)
            ]
            last.append(send(block, block, c_send.at[k, j], c_recv.at[k, j], partner))
    for copy in last:
        copy.wait_recv()
    for copy in started:
        copy.wait_send()


def spread_sems(sizes):
    _, slabs, layers = sizes
    dma = pltpu.SemaphoreType.DMA
    return [
        dma((layers - 1,)),
        dma((layers - 1,)),
        dma((slabs - 1, layers)),
        dma((slabs - 1, layers)),
        dma((slabs, layers)),
        dma((slabs, layers)),
    ]


def gather_kernel(sizes, x, out, local_sem, *sems):
    me = place()
    core, slab, layer = me
    keep = pltpu.make_async_copy(x, out.at[core, slab, layer], local_sem)
    keep.start()
    greet(sizes, me)
    spread(sizes, me, x, out, sems)
    keep.wait()


def gather(block, collective_id):
    sizes = dims()
    return pl.pallas_call(
        functools.partial(gather_kernel, sizes),
        out_shape=jax.ShapeDtypeStruct(sizes + block.shape, block.dtype),
        in_specs=[VM],
        out_specs=VM,
        scratch_shapes=[pltpu.SemaphoreType.DMA] + spread_sems(sizes),
        compiler_params=pltpu.CompilerParams(collective_id=collective_id, has_side_effects=True),
    )(block)


def reduce_kernel(sizes, x, out, first, half, second, quarter, third, *sems):
    cs, cr, ss, sr, zs, zr = sems[:6]
    _, slabs, layers = sizes
    me = place()
    core, slab, layer = me
    greet(sizes, me)

    def send(source, target, send_sem, recv_sem, device):
        copy = pltpu.make_async_remote_copy(
            src_ref=source,
            dst_ref=target,
            send_sem=send_sem,
            recv_sem=recv_sem,
            device_id=device,
            device_id_type=MESH,
        )
        copy.start()
        return copy

    order = list(range(1, slabs)) + [0]
    stage = {}
    for k in order:
        to = lax.rem(slab + k, slabs)
        stage[k] = send(
            x.at[1 - core, to], first.at[to], cs.at[k], cr.at[k], (slab, 2 * layer + 1 - core)
        )
    over = []
    for k in order:
        to = lax.rem(slab + k, slabs)
        stage[k].wait_recv()
        half[to] = x[core, to] + first[to]
        if k:
            over.append(
                send(half.at[to], second.at[k - 1], ss.at[k - 1], sr.at[k - 1], (to, 2 * layer + core))
            )
    total = half[slab]
    for k in range(1, slabs):
        over[k - 1].wait_recv()
        total = total + second[k - 1]
    quarter[...] = total
    along = []
    for k in range(1, layers):
        to = lax.rem(layer + k, layers)
        along.append(
            send(quarter.at[to], third.at[k - 1], zs.at[k - 1], zr.at[k - 1], (slab, 2 * to + core))
        )
    total = quarter[layer]
    for k in range(1, layers):
        along[k - 1].wait_recv()
        total = total + third[k - 1]
    out[core, slab, layer] = total
    spread(sizes, me, out.at[core, slab, layer], out, sems[6:])
    for copy in list(stage.values()) + over + along:
        copy.wait_send()


def all_reduce(rows, collective_id):
    sizes = dims()
    _, slabs, layers = sizes
    devices = 2 * slabs * layers
    count, width = rows.shape
    share = -(-count // devices)
    padded = jnp.pad(rows, ((0, share * devices - count), (0, 0)))
    block = (share, width)
    dma = pltpu.SemaphoreType.DMA
    buffers = [
        (slabs, layers) + block,
        (slabs, layers) + block,
        (slabs - 1, layers) + block,
        (layers,) + block,
        (layers - 1,) + block,
    ]
    result = pl.pallas_call(
        functools.partial(reduce_kernel, sizes),
        out_shape=jax.ShapeDtypeStruct(sizes + block, rows.dtype),
        in_specs=[VM],
        out_specs=VM,
        scratch_shapes=[pltpu.VMEM(item, rows.dtype) for item in buffers]
        + [
            dma((slabs,)),
            dma((slabs,)),
            dma((slabs - 1,)),
            dma((slabs - 1,)),
            dma((layers - 1,)),
            dma((layers - 1,)),
        ]
        + spread_sems(sizes),
        compiler_params=pltpu.CompilerParams(collective_id=collective_id, has_side_effects=True),
    )(padded.reshape(sizes + block))
    return result.reshape(share * devices, width)[:count]


def velocities(indices):
    spacing = 2.0 * VMAX / NVX
    first_index = indices // (NVX * NVX)
    second = indices // NVX % NVX
    third_index = indices % NVX
    coords = jnp.stack([first_index, second, third_index]).astype(jnp.float32)
    return -VMAX + (coords + 0.5) * spacing


def cell_state(vectors, coeffs):
    moments = lax.dot_general(vectors, coeffs, (((1,), (1,)), ((), ())), precision=PRECISE)
    density = jnp.maximum(moments[0], RHO_MIN)
    drift = moments[1:4] / density[None, :]
    temper = jnp.maximum((moments[4] / density - jnp.sum(drift * drift, axis=0)) / 3.0, TEMP_MIN)
    amplitude = density * (2.0 * math.pi * temper) ** (-1.5)
    zero = jnp.zeros_like(density)
    return jnp.stack([drift[0], drift[1], drift[2], -0.5 / temper, amplitude, zero, zero, zero])


def halves(values):
    high = values.astype(jnp.bfloat16)
    return high, (values - high.astype(jnp.float32)).astype(jnp.bfloat16)


def project_kernel(weight, cells, velocity, high_low, high, out):
    u1, u2, u3 = cells[:, 0:1], cells[:, 1:2], cells[:, 2:3]
    rate, amplitude = cells[:, 3:4], cells[:, 4:5]
    v1, v2, v3 = velocity[0:1, :], velocity[1:2, :], velocity[2:3, :]
    distance = (v1 - u1) ** 2 + (v2 - u2) ** 2 + (v3 - u3) ** 2
    top, rest = halves(jnp.exp(distance * rate))
    both = jnp.dot(top, high_low[...], preferred_element_type=jnp.float32)
    small = jnp.dot(rest, high[...], preferred_element_type=jnp.float32)
    rank = out.shape[1]
    out[...] = (both[:, :rank] + (both[:, rank:] + small)) * (amplitude * weight)


def project(cells, velocity, v_basis, weight):
    count = cells.shape[0]
    nodes, rank = v_basis.shape
    block = math.gcd(count, 256)
    high, low = halves(v_basis)
    return pl.pallas_call(
        functools.partial(project_kernel, weight),
        grid=(count // block,),
        out_shape=jax.ShapeDtypeStruct((count, rank), jnp.float32),
        in_specs=[
            pl.BlockSpec((block, 8), lambda i: (i, 0)),
            pl.BlockSpec((8, nodes), lambda i: (0, 0)),
            pl.BlockSpec((nodes, 2 * rank), lambda i: (0, 0)),
            pl.BlockSpec((nodes, rank), lambda i: (0, 0)),
        ],
        out_specs=pl.BlockSpec((block, rank), lambda i: (i, 0)),
    )(cells, velocity, jnp.concatenate([high, low], axis=1), high)


def fold_kernel(group, weight, cells, velocity, field_high_low, field_high, out):
    i = pl.program_id(0)

    @pl.when(i == 0)
    def _():
        out[...] = jnp.zeros_like(out)

    u1, u2, u3 = cells[0:1, :], cells[1:2, :], cells[2:3, :]
    rate = cells[3:4, :]
    nodes, rank = out.shape
    fast = jnp.exp(((velocity[0:group, 2:3] - u3) ** 2) * rate)
    pieces = []
    for start in range(0, nodes, group):
        v1 = velocity[start : start + 1, 0:1]
        v2 = velocity[start : start + 1, 1:2]
        slow = jnp.exp(((v1 - u1) ** 2 + (v2 - u2) ** 2) * rate)
        pieces.append(fast * slow)
    top, rest = halves(jnp.concatenate(pieces, axis=0))
    both = jnp.dot(top, field_high_low[...], preferred_element_type=jnp.float32)
    small = jnp.dot(rest, field_high[...], preferred_element_type=jnp.float32)
    out[...] += (both[:, :rank] + (both[:, rank:] + small)) * weight


def fold(cells, velocity, field, weight):
    count, rank = field.shape
    nodes = velocity.shape[0]
    block = math.gcd(count, 256)
    group = math.gcd(nodes, NVX)
    high, low = halves(field * cells[4][:, None])
    return pl.pallas_call(
        functools.partial(fold_kernel, group, weight),
        grid=(count // block,),
        out_shape=jax.ShapeDtypeStruct((nodes, rank), jnp.float32),
        in_specs=[
            pl.BlockSpec((8, block), lambda i: (0, i)),
            pl.BlockSpec((nodes, 8), lambda i: (0, 0)),
            pl.BlockSpec((block, 2 * rank), lambda i: (i, 0)),
            pl.BlockSpec((block, rank), lambda i: (i, 0)),
        ],
        out_specs=pl.BlockSpec((nodes, rank), lambda i: (0, 0)),
    )(cells, velocity, jnp.concatenate([high, low], axis=1), high)


def forward_slopes(grid, lengths):
    return [(jnp.roll(grid, -1, axis=d) - grid) * lengths[d] for d in range(3)]


def inverse_of(factor):
    identity = jnp.eye(factor.shape[0], dtype=jnp.float32)
    return jax.scipy.linalg.solve_triangular(factor, identity, lower=True)


def local(k_coeffs, v_basis):
    cells_x, cells_y, cells_z, rank = k_coeffs.shape
    slabs = lax.axis_size("slab")
    bricks = lax.axis_size("brick")
    lengths = (cells_x * slabs, cells_y * bricks, cells_z)
    cells = lengths[0] * lengths[1] * lengths[2]
    time_step = CFL / (VMAX * (lengths[0] + lengths[1] + lengths[2]))
    weight_x = 1.0 / cells
    weight_v = (2.0 * VMAX / NVX) ** 3
    nodes = v_basis.shape[0]
    slab, brick = lax.axis_index("slab"), lax.axis_index("brick")
    row_ids = (slab * bricks + brick) * nodes + jnp.arange(nodes, dtype=jnp.int32)
    velocity = velocities(row_ids)
    positive = jnp.maximum(velocity, 0.0)
    negative = jnp.minimum(velocity, 0.0)
    square = jnp.sum(velocity * velocity, axis=0)
    zero = jnp.zeros_like(square)
    ones = jnp.ones_like(square)
    weights = jnp.stack([ones, velocity[0], velocity[1], velocity[2], square, zero, zero, zero])
    partial = jnp.dot(weights, v_basis, precision=PRECISE) * weight_v
    packed = jnp.concatenate([partial, k_coeffs.reshape(-1, rank)], axis=0)
    gathered = gather(packed, 1)
    vectors = jnp.sum(gathered[:, :, :, :8], axis=(0, 1, 2))
    blocks = gathered[:, :, :, 8:].reshape(2, slabs, bricks // 2, cells_x, cells_y, cells_z, rank)
    grid = blocks.transpose(1, 3, 2, 0, 4, 5, 6).reshape(lengths + (rank,))
    flat = grid.reshape(cells, rank)

    rows = cell_state(vectors, flat)
    velocity_rows = jnp.pad(velocity, ((0, 5), (0, 0)))
    mproj_part = project(rows.T, velocity_rows, v_basis, weight_v)
    sides = jnp.concatenate([positive, negative], axis=0) * weight_v
    transport_part = lax.dot_general(
        sides[:, :, None] * v_basis[None],
        v_basis,
        (((1,), (0,)), ((), ())),
        precision=FAST,
    )
    summed = all_reduce(jnp.concatenate([mproj_part, transport_part.reshape(6 * rank, rank)]), 2)
    mproj = summed[:cells]
    transport = summed[cells:]

    fwd = forward_slopes(grid, lengths)
    back = [jnp.roll(item, 1, axis=d) for d, item in enumerate(fwd)]
    slopes = jnp.concatenate([item.reshape(cells, rank) for item in back + fwd], axis=1)
    flux = jnp.dot(slopes, transport, precision=FAST)
    advanced = flat - time_step * flux + COLLIDE * (mproj - flat)

    new_grid = advanced.reshape(lengths + (rank,))
    sides_new = [item.reshape(cells, rank) for item in forward_slopes(new_grid, lengths)]
    over_cells = (((0,), (0,)), ((), ()))
    gram = lax.dot_general(advanced, advanced, over_cells, precision=PRECISE) * weight_x
    raw = [
        lax.dot_general(advanced, item, over_cells, precision=FAST) * weight_x
        for item in sides_new + [mproj]
    ]
    factor = jnp.linalg.cholesky(gram)
    inverse = inverse_of(factor)
    plus = jnp.einsum("ab,kbc,dc->kad", inverse, jnp.stack(raw[:3]), inverse, precision=PRECISE)
    minus = -plus.transpose(0, 2, 1)
    projected = jnp.dot(inverse, raw[3], precision=PRECISE)
    both = jnp.concatenate([minus, plus], axis=0)
    middle = jnp.einsum("kab,cb->akc", both, factor, precision=PRECISE).reshape(rank, 6 * rank)
    hat = factor.T
    coupling_mid = (
        hat
        + time_step * jnp.dot(middle, transport, precision=PRECISE)
        - COLLIDE * (projected - hat)
    )

    velocity_columns = velocity_rows.T
    back_raw = fold(rows, velocity_columns, advanced, weight_x)
    back_proj = lax.dot_general(back_raw, inverse, (((1,), (1,)), ((), ())), precision=FAST)
    lnow = lax.dot_general(v_basis, coupling_mid, (((1,), (1,)), ((), ())), precision=FAST)
    turned = both.transpose(2, 0, 1).reshape(rank, 6 * rank)
    moved = jnp.dot(lnow, turned, precision=FAST)
    side_columns = jnp.concatenate([positive, negative], axis=0).T
    drift = sum(
        side_columns[:, k : k + 1] * moved[:, k * rank : (k + 1) * rank] for k in range(6)
    )
    lnew = lnow - time_step * drift + COLLIDE * (back_proj - lnow)
    gram_v = lax.dot_general(lnew, lnew, over_cells, precision=PRECISE) * weight_v
    gram_v = all_reduce(gram_v, 3)
    coupling = jnp.linalg.cholesky(gram_v)
    inverse_v = inverse_of(coupling)
    basis_v = lax.dot_general(lnew, inverse_v, (((1,), (1,)), ((), ())), precision=FAST)
    own = lax.dynamic_slice(
        new_grid,
        (slab * cells_x, brick * cells_y, 0, 0),
        (cells_x, cells_y, cells_z, rank),
    ).reshape(-1, rank)
    basis_x = lax.dot_general(own, inverse, (((1,), (1,)), ((), ())), precision=FAST)
    return basis_x.reshape(k_coeffs.shape), coupling, basis_v


def solution(mesh):
    return jax.shard_map(
        local,
        mesh=mesh,
        in_specs=(P("slab", "brick", None, None), P(("slab", "brick"), None)),
        out_specs=(P("slab", "brick", None, None), P(), P(("slab", "brick"), None)),
        check_vma=False,
    )
```

```python
import functools
import math

import jax
import jax.numpy as jnp
from jax import lax
from jax.experimental import pallas as pl
from jax.experimental.pallas import tpu as pltpu
from jax.sharding import PartitionSpec as P

NVX = 32

CFL = 0.9
VMAX = 6.0
COLLIDE = 0.3
RHO_MIN = 0.25
TEMP_MIN = 0.25
PRECISE = lax.Precision.HIGHEST
FAST = lax.Precision.HIGH
MESH = pl.DeviceIdType.MESH
VM = pl.BlockSpec(memory_space=pltpu.VMEM)


def dims():
    return 2, lax.axis_size("slab"), lax.axis_size("brick") // 2


def place():
    brick = lax.axis_index("brick")
    return lax.rem(brick, 2), lax.axis_index("slab"), lax.div(brick, 2)


def greet(sizes, me):
    _, slabs, layers = sizes
    core, slab, layer = me
    barrier = pltpu.get_barrier_semaphore()
    peers = [(slab, 2 * layer + 1 - core)]
    peers += [(lax.rem(slab + k, slabs), 2 * layer + core) for k in range(1, slabs)]
    peers += [(slab, 2 * lax.rem(layer + k, layers) + core) for k in range(1, layers)]
    for peer in peers:
        pl.semaphore_signal(barrier, inc=1, device_id=peer, device_id_type=MESH)
    pl.semaphore_wait(barrier, len(peers))


def spread(sizes, me, own, out, sems):
    _, slabs, layers = sizes
    core, slab, layer = me
    a_send, a_recv, b_send, b_recv, c_send, c_recv = sems
    partner = (slab, 2 * layer + 1 - core)
    started = []

    def send(source, target, send_sem, recv_sem, device):
        copy = pltpu.make_async_remote_copy(
            src_ref=source,
            dst_ref=target,
            send_sem=send_sem,
            recv_sem=recv_sem,
            device_id=device,
            device_id_type=MESH,
        )
        copy.start()
        started.append(copy)
        return copy

    def to_slabs(source, target, j):
        return [
            send(
                source,
                target,
                b_send.at[k - 1, j],
                b_recv.at[k - 1, j],
                (lax.rem(slab + k, slabs), 2 * layer + core),
            )
            for k in range(1, slabs)
        ]

    here = out.at[core, slab, layer]
    along = [
        send(own, here, a_send.at[k - 1], a_recv.at[k - 1], (slab, 2 * lax.rem(layer + k, layers) + core))
        for k in range(1, layers)
    ]
    crossing = [to_slabs(own, here, 0)]
    last = [send(own, here, c_send.at[0, 0], c_recv.at[0, 0], partner)]
    for j in range(1, layers):
        along[j - 1].wait_recv()
        block = out.at[core, slab, lax.rem(layer + layers - j, layers)]
        crossing.append(to_slabs(block, block, j))
        last.append(send(block, block, c_send.at[0, j], c_recv.at[0, j], partner))
    for j in range(layers):
        for k in range(1, slabs):
            crossing[j][k - 1].wait_recv()
            block = out.at[
                core, lax.rem(slab + slabs - k, slabs), lax.rem(layer + layers - j, layers)
            ]
            last.append(send(block, block, c_send.at[k, j], c_recv.at[k, j], partner))
    for copy in last:
        copy.wait_recv()
    for copy in started:
        copy.wait_send()


def spread_sems(sizes):
    _, slabs, layers = sizes
    dma = pltpu.SemaphoreType.DMA
    return [
        dma((layers - 1,)),
        dma((layers - 1,)),
        dma((slabs - 1, layers)),
        dma((slabs - 1, layers)),
        dma((slabs, layers)),
        dma((slabs, layers)),
    ]


def gather_kernel(sizes, x, out, local_sem, *sems):
    me = place()
    core, slab, layer = me
    keep = pltpu.make_async_copy(x, out.at[core, slab, layer], local_sem)
    keep.start()
    greet(sizes, me)
    spread(sizes, me, x, out, sems)
    keep.wait()


def gather(block, collective_id):
    sizes = dims()
    return pl.pallas_call(
        functools.partial(gather_kernel, sizes),
        out_shape=jax.ShapeDtypeStruct(sizes + block.shape, block.dtype),
        in_specs=[VM],
        out_specs=VM,
        scratch_shapes=[pltpu.SemaphoreType.DMA] + spread_sems(sizes),
        compiler_params=pltpu.CompilerParams(collective_id=collective_id, has_side_effects=True),
    )(block)


def reduce_kernel(sizes, x, out, first, half, second, quarter, third, *sems):
    cs, cr, ss, sr, zs, zr = sems[:6]
    _, slabs, layers = sizes
    me = place()
    core, slab, layer = me
    greet(sizes, me)

    def send(source, target, send_sem, recv_sem, device):
        copy = pltpu.make_async_remote_copy(
            src_ref=source,
            dst_ref=target,
            send_sem=send_sem,
            recv_sem=recv_sem,
            device_id=device,
            device_id_type=MESH,
        )
        copy.start()
        return copy

    order = list(range(1, slabs)) + [0]
    stage = {}
    for k in order:
        to = lax.rem(slab + k, slabs)
        stage[k] = send(
            x.at[1 - core, to], first.at[to], cs.at[k], cr.at[k], (slab, 2 * layer + 1 - core)
        )
    over = []
    for k in order:
        to = lax.rem(slab + k, slabs)
        stage[k].wait_recv()
        half[to] = x[core, to] + first[to]
        if k:
            over.append(
                send(half.at[to], second.at[k - 1], ss.at[k - 1], sr.at[k - 1], (to, 2 * layer + core))
            )
    total = half[slab]
    for k in range(1, slabs):
        over[k - 1].wait_recv()
        total = total + second[k - 1]
    quarter[...] = total
    along = []
    for k in range(1, layers):
        to = lax.rem(layer + k, layers)
        along.append(
            send(quarter.at[to], third.at[k - 1], zs.at[k - 1], zr.at[k - 1], (slab, 2 * to + core))
        )
    total = quarter[layer]
    for k in range(1, layers):
        along[k - 1].wait_recv()
        total = total + third[k - 1]
    out[core, slab, layer] = total
    spread(sizes, me, out.at[core, slab, layer], out, sems[6:])
    for copy in list(stage.values()) + over + along:
        copy.wait_send()


def all_reduce(rows, collective_id):
    sizes = dims()
    _, slabs, layers = sizes
    devices = 2 * slabs * layers
    count, width = rows.shape
    share = -(-count // devices)
    padded = jnp.pad(rows, ((0, share * devices - count), (0, 0)))
    block = (share, width)
    dma = pltpu.SemaphoreType.DMA
    buffers = [
        (slabs, layers) + block,
        (slabs, layers) + block,
        (slabs - 1, layers) + block,
        (layers,) + block,
        (layers - 1,) + block,
    ]
    result = pl.pallas_call(
        functools.partial(reduce_kernel, sizes),
        out_shape=jax.ShapeDtypeStruct(sizes + block, rows.dtype),
        in_specs=[VM],
        out_specs=VM,
        scratch_shapes=[pltpu.VMEM(item, rows.dtype) for item in buffers]
        + [
            dma((slabs,)),
            dma((slabs,)),
            dma((slabs - 1,)),
            dma((slabs - 1,)),
            dma((layers - 1,)),
            dma((layers - 1,)),
        ]
        + spread_sems(sizes),
        compiler_params=pltpu.CompilerParams(collective_id=collective_id, has_side_effects=True),
    )(padded.reshape(sizes + block))
    return result.reshape(share * devices, width)[:count]


def velocities(indices):
    spacing = 2.0 * VMAX / NVX
    first_index = indices // (NVX * NVX)
    second = indices // NVX % NVX
    third_index = indices % NVX
    coords = jnp.stack([first_index, second, third_index]).astype(jnp.float32)
    return -VMAX + (coords + 0.5) * spacing


def cell_state(vectors, coeffs):
    moments = lax.dot_general(vectors, coeffs, (((1,), (1,)), ((), ())), precision=PRECISE)
    density = jnp.maximum(moments[0], RHO_MIN)
    drift = moments[1:4] / density[None, :]
    temper = jnp.maximum((moments[4] / density - jnp.sum(drift * drift, axis=0)) / 3.0, TEMP_MIN)
    amplitude = density * (2.0 * math.pi * temper) ** (-1.5)
    zero = jnp.zeros_like(density)
    return jnp.stack([drift[0], drift[1], drift[2], -0.5 / temper, amplitude, zero, zero, zero])


def halves(values):
    high = values.astype(jnp.bfloat16)
    return high, (values - high.astype(jnp.float32)).astype(jnp.bfloat16)


def split_into(values, high_low):
    high, low = halves(values)
    rank = values.shape[1]
    high_low[:, :rank] = high
    high_low[:, rank:] = low


def project_kernel(weight, cells, velocity, v_basis, out, high_low):
    @pl.when(pl.program_id(0) == 0)
    def _():
        split_into(v_basis[...], high_low)

    u1, u2, u3 = cells[:, 0:1], cells[:, 1:2], cells[:, 2:3]
    rate, amplitude = cells[:, 3:4], cells[:, 4:5]
    v1, v2, v3 = velocity[0:1, :], velocity[1:2, :], velocity[2:3, :]
    distance = (v1 - u1) ** 2 + (v2 - u2) ** 2 + (v3 - u3) ** 2
    top, rest = halves(jnp.exp(distance * rate))
    both = jnp.dot(top, high_low[...], preferred_element_type=jnp.float32)
    rank = out.shape[1]
    small = jnp.dot(rest, high_low[:, :rank], preferred_element_type=jnp.float32)
    out[...] = (both[:, :rank] + (both[:, rank:] + small)) * (amplitude * weight)


def project(cells, velocity, v_basis, weight):
    count = cells.shape[0]
    nodes, rank = v_basis.shape
    block = math.gcd(count, 256)
    return pl.pallas_call(
        functools.partial(project_kernel, weight),
        grid=(count // block,),
        out_shape=jax.ShapeDtypeStruct((count, rank), jnp.float32),
        in_specs=[
            pl.BlockSpec((block, 8), lambda i: (i, 0)),
            pl.BlockSpec((8, nodes), lambda i: (0, 0)),
            pl.BlockSpec((nodes, rank), lambda i: (0, 0)),
        ],
        out_specs=pl.BlockSpec((block, rank), lambda i: (i, 0)),
        scratch_shapes=[pltpu.VMEM((nodes, 2 * rank), jnp.bfloat16)],
    )(cells, velocity, v_basis)


def fold_kernel(group, weight, cells, velocity, field, out, high_low):
    i = pl.program_id(0)

    @pl.when(i == 0)
    def _():
        out[...] = jnp.zeros_like(out)

    split_into(field[...], high_low)
    u1, u2, u3 = cells[0:1, :], cells[1:2, :], cells[2:3, :]
    rate = cells[3:4, :]
    nodes, rank = out.shape
    fast = jnp.exp(((velocity[0:group, 2:3] - u3) ** 2) * rate)
    pieces = []
    for start in range(0, nodes, group):
        v1 = velocity[start : start + 1, 0:1]
        v2 = velocity[start : start + 1, 1:2]
        slow = jnp.exp(((v1 - u1) ** 2 + (v2 - u2) ** 2) * rate)
        pieces.append(fast * slow)
    top, rest = halves(jnp.concatenate(pieces, axis=0))
    both = jnp.dot(top, high_low[...], preferred_element_type=jnp.float32)
    small = jnp.dot(rest, high_low[:, :rank], preferred_element_type=jnp.float32)
    out[...] += (both[:, :rank] + (both[:, rank:] + small)) * weight


def fold(cells, velocity, field, weight):
    count, rank = field.shape
    nodes = velocity.shape[0]
    block = math.gcd(count, 256)
    group = math.gcd(nodes, NVX)
    return pl.pallas_call(
        functools.partial(fold_kernel, group, weight),
        grid=(count // block,),
        out_shape=jax.ShapeDtypeStruct((nodes, rank), jnp.float32),
        in_specs=[
            pl.BlockSpec((8, block), lambda i: (0, i)),
            pl.BlockSpec((nodes, 8), lambda i: (0, 0)),
            pl.BlockSpec((block, rank), lambda i: (i, 0)),
        ],
        out_specs=pl.BlockSpec((nodes, rank), lambda i: (0, 0)),
        scratch_shapes=[pltpu.VMEM((block, 2 * rank), jnp.bfloat16)],
    )(cells, velocity, field * cells[4][:, None])


def forward_slopes(grid, lengths):
    return [(jnp.roll(grid, -1, axis=d) - grid) * lengths[d] for d in range(3)]


def inverse_kernel(factor, out):
    size = out.shape[0]
    row = lax.broadcasted_iota(jnp.int32, out.shape, 0)
    column = lax.broadcasted_iota(jnp.int32, out.shape, 1)
    lower = factor[...]
    inverse = jnp.where(row == column, 1.0 / lower, 0.0)
    shift = 0
    while (1 << shift) < size:
        row_block, column_block = row >> shift, column >> shift
        below = (row_block == column_block + 1) & ((column_block & 1) == 0)
        joint = jnp.where(below, lower, 0.0)
        joint = jnp.dot(inverse, joint, precision=PRECISE, preferred_element_type=jnp.float32)
        inverse = inverse - jnp.dot(
            joint, inverse, precision=PRECISE, preferred_element_type=jnp.float32
        )
        shift += 1
    out[...] = inverse


def inverse_of(factor):
    return pl.pallas_call(
        inverse_kernel,
        out_shape=jax.ShapeDtypeStruct(factor.shape, factor.dtype),
        in_specs=[VM],
        out_specs=VM,
    )(factor)


def small_kernel(sizes, x, out, first, second, *sems):
    ms, mr, zs, zr, gs, gr = sems
    _, slabs, layers = sizes
    core, slab, layer = place()
    members = 2 * slabs
    me = 2 * slab + core

    def member(k):
        to = lax.rem(me + k, members)
        return to, (lax.div(to, 2), 2 * layer + lax.rem(to, 2))

    def across(k):
        return (slab, 2 * lax.rem(layer + k, layers) + core)

    barrier = pltpu.get_barrier_semaphore()
    peers = [member(k)[1] for k in range(1, members)] + [across(k) for k in range(1, layers)]
    for peer in peers:
        pl.semaphore_signal(barrier, inc=1, device_id=peer, device_id_type=MESH)
    pl.semaphore_wait(barrier, len(peers))

    def send(source, target, send_sem, recv_sem, device):
        copy = pltpu.make_async_remote_copy(
            src_ref=source,
            dst_ref=target,
            send_sem=send_sem,
            recv_sem=recv_sem,
            device_id=device,
            device_id_type=MESH,
        )
        copy.start()
        return copy

    scatter = []
    for k in range(1, members):
        to, device = member(k)
        scatter.append(send(x.at[to], first.at[k - 1], ms.at[k - 1], mr.at[k - 1], device))
    total = x[me]
    for k in range(1, members):
        scatter[k - 1].wait_recv()
        total = total + first[k - 1]
    second[layer] = total
    mine = second.at[layer]
    cross = [
        send(mine, mine, zs.at[k - 1], zr.at[k - 1], across(k)) for k in range(1, layers)
    ]
    for copy in cross:
        copy.wait_recv()
    total = second[0]
    for k in range(1, layers):
        total = total + second[k]
    out[me] = total
    mine = out.at[me]
    collect = [
        send(mine, mine, gs.at[k - 1], gr.at[k - 1], member(k)[1]) for k in range(1, members)
    ]
    for copy in collect:
        copy.wait_recv()
    for copy in scatter + cross + collect:
        copy.wait_send()


def small_all_reduce(rows, collective_id):
    sizes = dims()
    _, slabs, layers = sizes
    members = 2 * slabs
    count, width = rows.shape
    share = -(-count // members)
    padded = jnp.pad(rows, ((0, share * members - count), (0, 0)))
    dma = pltpu.SemaphoreType.DMA
    result = pl.pallas_call(
        functools.partial(small_kernel, sizes),
        out_shape=jax.ShapeDtypeStruct((members, share, width), rows.dtype),
        in_specs=[VM],
        out_specs=VM,
        scratch_shapes=[
            pltpu.VMEM((members - 1, share, width), rows.dtype),
            pltpu.VMEM((layers, share, width), rows.dtype),
            dma((members - 1,)),
            dma((members - 1,)),
            dma((layers - 1,)),
            dma((layers - 1,)),
            dma((members - 1,)),
            dma((members - 1,)),
        ],
        compiler_params=pltpu.CompilerParams(collective_id=collective_id, has_side_effects=True),
    )(padded.reshape(members, share, width))
    return result.reshape(share * members, width)[:count]


def local(k_coeffs, v_basis):
    cells_x, cells_y, cells_z, rank = k_coeffs.shape
    slabs = lax.axis_size("slab")
    bricks = lax.axis_size("brick")
    lengths = (cells_x * slabs, cells_y * bricks, cells_z)
    cells = lengths[0] * lengths[1] * lengths[2]
    time_step = CFL / (VMAX * (lengths[0] + lengths[1] + lengths[2]))
    weight_x = 1.0 / cells
    weight_v = (2.0 * VMAX / NVX) ** 3
    nodes = v_basis.shape[0]
    slab, brick = lax.axis_index("slab"), lax.axis_index("brick")
    row_ids = (slab * bricks + brick) * nodes + jnp.arange(nodes, dtype=jnp.int32)
    velocity = velocities(row_ids)
    positive = jnp.maximum(velocity, 0.0)
    negative = jnp.minimum(velocity, 0.0)
    square = jnp.sum(velocity * velocity, axis=0)
    zero = jnp.zeros_like(square)
    ones = jnp.ones_like(square)
    weights = jnp.stack([ones, velocity[0], velocity[1], velocity[2], square, zero, zero, zero])
    partial = jnp.dot(weights, v_basis, precision=PRECISE) * weight_v
    packed = jnp.concatenate([partial, k_coeffs.reshape(-1, rank)], axis=0)
    gathered = gather(packed, 1)
    vectors = jnp.sum(gathered[:, :, :, :8], axis=(0, 1, 2))
    blocks = gathered[:, :, :, 8:].reshape(2, slabs, bricks // 2, cells_x, cells_y, cells_z, rank)
    grid = blocks.transpose(1, 3, 2, 0, 4, 5, 6).reshape(lengths + (rank,))
    flat = grid.reshape(cells, rank)

    rows = cell_state(vectors, flat)
    velocity_rows = jnp.pad(velocity, ((0, 5), (0, 0)))
    mproj_part = project(rows.T, velocity_rows, v_basis, weight_v)
    sides = jnp.concatenate([positive, negative], axis=0) * weight_v
    transport_part = lax.dot_general(
        sides[:, :, None] * v_basis[None],
        v_basis,
        (((1,), (0,)), ((), ())),
        precision=FAST,
    )
    summed = all_reduce(jnp.concatenate([mproj_part, transport_part.reshape(6 * rank, rank)]), 2)
    mproj = summed[:cells]
    transport = summed[cells:]

    fwd = forward_slopes(grid, lengths)
    back = [jnp.roll(item, 1, axis=d) for d, item in enumerate(fwd)]
    slopes = jnp.concatenate([item.reshape(cells, rank) for item in back + fwd], axis=1)
    flux = jnp.dot(slopes, transport, precision=FAST)
    advanced = flat - time_step * flux + COLLIDE * (mproj - flat)

    new_grid = advanced.reshape(lengths + (rank,))
    sides_new = [item.reshape(cells, rank) for item in forward_slopes(new_grid, lengths)]
    over_cells = (((0,), (0,)), ((), ()))
    gram = lax.dot_general(advanced, advanced, over_cells, precision=PRECISE) * weight_x
    raw = [
        lax.dot_general(advanced, item, over_cells, precision=FAST) * weight_x
        for item in sides_new + [mproj]
    ]
    factor = lax.linalg.cholesky(gram, symmetrize_input=False)
    inverse = inverse_of(factor)
    plus = jnp.einsum("ab,kbc,dc->kad", inverse, jnp.stack(raw[:3]), inverse, precision=PRECISE)
    minus = -plus.transpose(0, 2, 1)
    projected = jnp.dot(inverse, raw[3], precision=PRECISE)
    both = jnp.concatenate([minus, plus], axis=0)
    middle = jnp.einsum("kab,cb->akc", both, factor, precision=PRECISE).reshape(rank, 6 * rank)
    hat = factor.T
    coupling_mid = (
        hat
        + time_step * jnp.dot(middle, transport, precision=PRECISE)
        - COLLIDE * (projected - hat)
    )

    velocity_columns = velocity_rows.T
    back_raw = fold(rows, velocity_columns, advanced, weight_x)
    back_proj = lax.dot_general(back_raw, inverse, (((1,), (1,)), ((), ())), precision=FAST)
    lnow = lax.dot_general(v_basis, coupling_mid, (((1,), (1,)), ((), ())), precision=FAST)
    turned = both.transpose(2, 0, 1).reshape(rank, 6 * rank)
    moved = jnp.dot(lnow, turned, precision=FAST)
    side_columns = jnp.concatenate([positive, negative], axis=0).T
    drift = sum(
        side_columns[:, k : k + 1] * moved[:, k * rank : (k + 1) * rank] for k in range(6)
    )
    lnew = lnow - time_step * drift + COLLIDE * (back_proj - lnow)
    gram_v = lax.dot_general(lnew, lnew, over_cells, precision=PRECISE) * weight_v
    gram_v = small_all_reduce(gram_v, 3)
    coupling = lax.linalg.cholesky(gram_v, symmetrize_input=False)
    inverse_v = inverse_of(coupling)
    basis_v = lax.dot_general(lnew, inverse_v, (((1,), (1,)), ((), ())), precision=FAST)
    own = lax.dynamic_slice(
        new_grid,
        (slab * cells_x, brick * cells_y, 0, 0),
        (cells_x, cells_y, cells_z, rank),
    ).reshape(-1, rank)
    basis_x = lax.dot_general(own, inverse, (((1,), (1,)), ((), ())), precision=FAST)
    return basis_x.reshape(k_coeffs.shape), coupling, basis_v


def solution(mesh):
    return jax.shard_map(
        local,
        mesh=mesh,
        in_specs=(P("slab", "brick", None, None), P(("slab", "brick"), None)),
        out_specs=(P("slab", "brick", None, None), P(), P(("slab", "brick"), None)),
        check_vma=False,
    )
```

```python
import functools
import math

import jax
import jax.numpy as jnp
from jax import lax
from jax.experimental import pallas as pl
from jax.experimental.pallas import tpu as pltpu
from jax.sharding import PartitionSpec as P

NVX = 32

CFL = 0.9
VMAX = 6.0
COLLIDE = 0.3
RHO_MIN = 0.25
TEMP_MIN = 0.25
PRECISE = lax.Precision.HIGHEST
FAST = lax.Precision.HIGH
MESH = pl.DeviceIdType.MESH
VM = pl.BlockSpec(memory_space=pltpu.VMEM)


def dims():
    return 2, lax.axis_size("slab"), lax.axis_size("brick") // 2


def place():
    brick = lax.axis_index("brick")
    return lax.rem(brick, 2), lax.axis_index("slab"), lax.div(brick, 2)


def greet(sizes, me):
    _, slabs, layers = sizes
    core, slab, layer = me
    barrier = pltpu.get_barrier_semaphore()
    peers = [(slab, 2 * layer + 1 - core)]
    peers += [(lax.rem(slab + k, slabs), 2 * layer + core) for k in range(1, slabs)]
    peers += [(slab, 2 * lax.rem(layer + k, layers) + core) for k in range(1, layers)]
    for peer in peers:
        pl.semaphore_signal(barrier, inc=1, device_id=peer, device_id_type=MESH)
    pl.semaphore_wait(barrier, len(peers))


def spread(sizes, me, own, out, sems):
    _, slabs, layers = sizes
    core, slab, layer = me
    a_send, a_recv, b_send, b_recv, c_send, c_recv = sems
    partner = (slab, 2 * layer + 1 - core)
    started = []

    def send(source, target, send_sem, recv_sem, device):
        copy = pltpu.make_async_remote_copy(
            src_ref=source,
            dst_ref=target,
            send_sem=send_sem,
            recv_sem=recv_sem,
            device_id=device,
            device_id_type=MESH,
        )
        copy.start()
        started.append(copy)
        return copy

    def to_slabs(source, target, j):
        return [
            send(
                source,
                target,
                b_send.at[k - 1, j],
                b_recv.at[k - 1, j],
                (lax.rem(slab + k, slabs), 2 * layer + core),
            )
            for k in range(1, slabs)
        ]

    here = out.at[core, slab, layer]
    along = [
        send(own, here, a_send.at[k - 1], a_recv.at[k - 1], (slab, 2 * lax.rem(layer + k, layers) + core))
        for k in range(1, layers)
    ]
    crossing = [to_slabs(own, here, 0)]
    last = [send(own, here, c_send.at[0, 0], c_recv.at[0, 0], partner)]
    for j in range(1, layers):
        along[j - 1].wait_recv()
        block = out.at[core, slab, lax.rem(layer + layers - j, layers)]
        crossing.append(to_slabs(block, block, j))
        last.append(send(block, block, c_send.at[0, j], c_recv.at[0, j], partner))
    for j in range(layers):
        for k in range(1, slabs):
            crossing[j][k - 1].wait_recv()
            block = out.at[
                core, lax.rem(slab + slabs - k, slabs), lax.rem(layer + layers - j, layers)
            ]
            last.append(send(block, block, c_send.at[k, j], c_recv.at[k, j], partner))
    for copy in last:
        copy.wait_recv()
    for copy in started:
        copy.wait_send()


def spread_sems(sizes):
    _, slabs, layers = sizes
    dma = pltpu.SemaphoreType.DMA
    return [
        dma((layers - 1,)),
        dma((layers - 1,)),
        dma((slabs - 1, layers)),
        dma((slabs - 1, layers)),
        dma((slabs, layers)),
        dma((slabs, layers)),
    ]


def gather_kernel(sizes, x, out, local_sem, *sems):
    me = place()
    core, slab, layer = me
    keep = pltpu.make_async_copy(x, out.at[core, slab, layer], local_sem)
    keep.start()
    greet(sizes, me)
    spread(sizes, me, x, out, sems)
    keep.wait()


def gather(block, collective_id):
    sizes = dims()
    return pl.pallas_call(
        functools.partial(gather_kernel, sizes),
        out_shape=jax.ShapeDtypeStruct(sizes + block.shape, block.dtype),
        in_specs=[VM],
        out_specs=VM,
        scratch_shapes=[pltpu.SemaphoreType.DMA] + spread_sems(sizes),
        compiler_params=pltpu.CompilerParams(collective_id=collective_id, has_side_effects=True),
    )(block)


def reduce_kernel(sizes, x, out, first, half, second, quarter, third, *sems):
    cs, cr, ss, sr, zs, zr = sems[:6]
    _, slabs, layers = sizes
    me = place()
    core, slab, layer = me
    greet(sizes, me)

    def send(source, target, send_sem, recv_sem, device):
        copy = pltpu.make_async_remote_copy(
            src_ref=source,
            dst_ref=target,
            send_sem=send_sem,
            recv_sem=recv_sem,
            device_id=device,
            device_id_type=MESH,
        )
        copy.start()
        return copy

    slab_order = list(range(1, slabs)) + [0]
    layer_order = list(range(1, layers)) + [0]
    partner = (slab, 2 * layer + 1 - core)
    stage, over, along = {}, {}, {}
    for n in layer_order:
        level = lax.rem(layer + n, layers)
        for k in slab_order:
            to = lax.rem(slab + k, slabs)
            stage[k, n] = send(
                x.at[1 - core, to, level], first.at[to, level], cs.at[k, n], cr.at[k, n], partner
            )

    def join_cores(n):
        level = lax.rem(layer + n, layers)
        for k in slab_order:
            to = lax.rem(slab + k, slabs)
            stage[k, n].wait_recv()
            half[to, level] = x[core, to, level] + first[to, level]
            if k:
                over[k, n] = send(
                    half.at[to, level],
                    second.at[k - 1, level],
                    ss.at[k - 1, n],
                    sr.at[k - 1, n],
                    (to, 2 * layer + core),
                )

    def join_slabs(n):
        level = lax.rem(layer + n, layers)
        total = half[slab, level]
        for k in range(1, slabs):
            over[k, n].wait_recv()
            total = total + second[k - 1, level]
        quarter[level] = total
        if n:
            along[n] = send(
                quarter.at[level],
                third.at[n - 1],
                zs.at[n - 1],
                zr.at[n - 1],
                (slab, 2 * level + core),
            )

    join_cores(layer_order[0])
    for place_in_order, n in enumerate(layer_order):
        if place_in_order + 1 < layers:
            join_cores(layer_order[place_in_order + 1])
        join_slabs(n)
    total = quarter[layer]
    for n in range(1, layers):
        along[n].wait_recv()
        total = total + third[n - 1]
    out[core, slab, layer] = total
    spread(sizes, me, out.at[core, slab, layer], out, sems[6:])
    for copy in list(stage.values()) + list(over.values()) + list(along.values()):
        copy.wait_send()


def all_reduce(rows, collective_id):
    sizes = dims()
    _, slabs, layers = sizes
    devices = 2 * slabs * layers
    count, width = rows.shape
    share = -(-count // devices)
    padded = jnp.pad(rows, ((0, share * devices - count), (0, 0)))
    block = (share, width)
    dma = pltpu.SemaphoreType.DMA
    buffers = [
        (slabs, layers) + block,
        (slabs, layers) + block,
        (slabs - 1, layers) + block,
        (layers,) + block,
        (layers - 1,) + block,
    ]
    result = pl.pallas_call(
        functools.partial(reduce_kernel, sizes),
        out_shape=jax.ShapeDtypeStruct(sizes + block, rows.dtype),
        in_specs=[VM],
        out_specs=VM,
        scratch_shapes=[pltpu.VMEM(item, rows.dtype) for item in buffers]
        + [
            dma((slabs, layers)),
            dma((slabs, layers)),
            dma((slabs - 1, layers)),
            dma((slabs - 1, layers)),
            dma((layers - 1,)),
            dma((layers - 1,)),
        ]
        + spread_sems(sizes),
        compiler_params=pltpu.CompilerParams(collective_id=collective_id, has_side_effects=True),
    )(padded.reshape(sizes + block))
    return result.reshape(share * devices, width)[:count]


def velocities(indices):
    spacing = 2.0 * VMAX / NVX
    first_index = indices // (NVX * NVX)
    second = indices // NVX % NVX
    third_index = indices % NVX
    coords = jnp.stack([first_index, second, third_index]).astype(jnp.float32)
    return -VMAX + (coords + 0.5) * spacing


def cell_state(vectors, coeffs):
    moments = lax.dot_general(vectors, coeffs, (((1,), (1,)), ((), ())), precision=PRECISE)
    density = jnp.maximum(moments[0], RHO_MIN)
    drift = moments[1:4] / density[None, :]
    temper = jnp.maximum((moments[4] / density - jnp.sum(drift * drift, axis=0)) / 3.0, TEMP_MIN)
    amplitude = density * (2.0 * math.pi * temper) ** (-1.5)
    zero = jnp.zeros_like(density)
    return jnp.stack([drift[0], drift[1], drift[2], -0.5 / temper, amplitude, zero, zero, zero])


def halves(values):
    high = values.astype(jnp.bfloat16)
    return high, (values - high.astype(jnp.float32)).astype(jnp.bfloat16)


def split_into(values, high_low):
    high, low = halves(values)
    rank = values.shape[1]
    high_low[:, :rank] = high
    high_low[:, rank:] = low


def project_kernel(weight, cells, velocity, v_basis, out, high_low):
    @pl.when(pl.program_id(0) == 0)
    def _():
        split_into(v_basis[...], high_low)

    u1, u2, u3 = cells[:, 0:1], cells[:, 1:2], cells[:, 2:3]
    rate, amplitude = cells[:, 3:4], cells[:, 4:5]
    v1, v2, v3 = velocity[0:1, :], velocity[1:2, :], velocity[2:3, :]
    distance = (v1 - u1) ** 2 + (v2 - u2) ** 2 + (v3 - u3) ** 2
    top, rest = halves(jnp.exp(distance * rate))
    both = jnp.dot(top, high_low[...], preferred_element_type=jnp.float32)
    rank = out.shape[1]
    small = jnp.dot(rest, high_low[:, :rank], preferred_element_type=jnp.float32)
    out[...] = (both[:, :rank] + (both[:, rank:] + small)) * (amplitude * weight)


def project(cells, velocity, v_basis, weight):
    count = cells.shape[0]
    nodes, rank = v_basis.shape
    block = math.gcd(count, 512)
    return pl.pallas_call(
        functools.partial(project_kernel, weight),
        grid=(count // block,),
        out_shape=jax.ShapeDtypeStruct((count, rank), jnp.float32),
        in_specs=[
            pl.BlockSpec((block, 8), lambda i: (i, 0)),
            pl.BlockSpec((8, nodes), lambda i: (0, 0)),
            pl.BlockSpec((nodes, rank), lambda i: (0, 0)),
        ],
        out_specs=pl.BlockSpec((block, rank), lambda i: (i, 0)),
        scratch_shapes=[pltpu.VMEM((nodes, 2 * rank), jnp.bfloat16)],
    )(cells, velocity, v_basis)


def fold_kernel(group, weight, cells, velocity, field, out, high_low):
    i = pl.program_id(0)

    @pl.when(i == 0)
    def _():
        out[...] = jnp.zeros_like(out)

    split_into(field[...], high_low)
    u1, u2, u3 = cells[0:1, :], cells[1:2, :], cells[2:3, :]
    rate = cells[3:4, :]
    nodes, rank = out.shape
    fast = jnp.exp(((velocity[0:group, 2:3] - u3) ** 2) * rate)
    pieces = []
    for start in range(0, nodes, group):
        v1 = velocity[start : start + 1, 0:1]
        v2 = velocity[start : start + 1, 1:2]
        slow = jnp.exp(((v1 - u1) ** 2 + (v2 - u2) ** 2) * rate)
        pieces.append(fast * slow)
    top, rest = halves(jnp.concatenate(pieces, axis=0))
    both = jnp.dot(top, high_low[...], preferred_element_type=jnp.float32)
    small = jnp.dot(rest, high_low[:, :rank], preferred_element_type=jnp.float32)
    out[...] += (both[:, :rank] + (both[:, rank:] + small)) * weight


def fold(cells, velocity, field, weight):
    count, rank = field.shape
    nodes = velocity.shape[0]
    block = math.gcd(count, 512)
    group = math.gcd(nodes, NVX)
    return pl.pallas_call(
        functools.partial(fold_kernel, group, weight),
        grid=(count // block,),
        out_shape=jax.ShapeDtypeStruct((nodes, rank), jnp.float32),
        in_specs=[
            pl.BlockSpec((8, block), lambda i: (0, i)),
            pl.BlockSpec((nodes, 8), lambda i: (0, 0)),
            pl.BlockSpec((block, rank), lambda i: (i, 0)),
        ],
        out_specs=pl.BlockSpec((nodes, rank), lambda i: (0, 0)),
        scratch_shapes=[pltpu.VMEM((block, 2 * rank), jnp.bfloat16)],
    )(cells, velocity, field * cells[4][:, None])


def forward_slopes(grid, lengths):
    return [(jnp.roll(grid, -1, axis=d) - grid) * lengths[d] for d in range(3)]


def inverse_kernel(factor, out):
    size = out.shape[0]
    row = lax.broadcasted_iota(jnp.int32, out.shape, 0)
    column = lax.broadcasted_iota(jnp.int32, out.shape, 1)
    lower = factor[...]
    inverse = jnp.where(row == column, 1.0 / lower, 0.0)
    shift = 0
    while (1 << shift) < size:
        row_block, column_block = row >> shift, column >> shift
        below = (row_block == column_block + 1) & ((column_block & 1) == 0)
        joint = jnp.where(below, lower, 0.0)
        joint = jnp.dot(inverse, joint, precision=PRECISE, preferred_element_type=jnp.float32)
        inverse = inverse - jnp.dot(
            joint, inverse, precision=PRECISE, preferred_element_type=jnp.float32
        )
        shift += 1
    out[...] = inverse


def inverse_of(factor):
    return pl.pallas_call(
        inverse_kernel,
        out_shape=jax.ShapeDtypeStruct(factor.shape, factor.dtype),
        in_specs=[VM],
        out_specs=VM,
    )(factor)


def small_kernel(sizes, x, out, first, second, *sems):
    ms, mr, zs, zr, gs, gr = sems
    _, slabs, layers = sizes
    core, slab, layer = place()
    members = 2 * slabs
    me = 2 * slab + core

    def member(k):
        to = lax.rem(me + k, members)
        return to, (lax.div(to, 2), 2 * layer + lax.rem(to, 2))

    def across(k):
        return (slab, 2 * lax.rem(layer + k, layers) + core)

    barrier = pltpu.get_barrier_semaphore()
    peers = [member(k)[1] for k in range(1, members)] + [across(k) for k in range(1, layers)]
    for peer in peers:
        pl.semaphore_signal(barrier, inc=1, device_id=peer, device_id_type=MESH)
    pl.semaphore_wait(barrier, len(peers))

    def send(source, target, send_sem, recv_sem, device):
        copy = pltpu.make_async_remote_copy(
            src_ref=source,
            dst_ref=target,
            send_sem=send_sem,
            recv_sem=recv_sem,
            device_id=device,
            device_id_type=MESH,
        )
        copy.start()
        return copy

    scatter = []
    for k in range(1, members):
        to, device = member(k)
        scatter.append(send(x.at[to], first.at[k - 1], ms.at[k - 1], mr.at[k - 1], device))
    total = x[me]
    for k in range(1, members):
        scatter[k - 1].wait_recv()
        total = total + first[k - 1]
    second[layer] = total
    mine = second.at[layer]
    cross = [
        send(mine, mine, zs.at[k - 1], zr.at[k - 1], across(k)) for k in range(1, layers)
    ]
    for copy in cross:
        copy.wait_recv()
    total = second[0]
    for k in range(1, layers):
        total = total + second[k]
    out[me] = total
    mine = out.at[me]
    collect = [
        send(mine, mine, gs.at[k - 1], gr.at[k - 1], member(k)[1]) for k in range(1, members)
    ]
    for copy in collect:
        copy.wait_recv()
    for copy in scatter + cross + collect:
        copy.wait_send()


def small_all_reduce(rows, collective_id):
    sizes = dims()
    _, slabs, layers = sizes
    members = 2 * slabs
    count, width = rows.shape
    share = -(-count // members)
    padded = jnp.pad(rows, ((0, share * members - count), (0, 0)))
    dma = pltpu.SemaphoreType.DMA
    result = pl.pallas_call(
        functools.partial(small_kernel, sizes),
        out_shape=jax.ShapeDtypeStruct((members, share, width), rows.dtype),
        in_specs=[VM],
        out_specs=VM,
        scratch_shapes=[
            pltpu.VMEM((members - 1, share, width), rows.dtype),
            pltpu.VMEM((layers, share, width), rows.dtype),
            dma((members - 1,)),
            dma((members - 1,)),
            dma((layers - 1,)),
            dma((layers - 1,)),
            dma((members - 1,)),
            dma((members - 1,)),
        ],
        compiler_params=pltpu.CompilerParams(collective_id=collective_id, has_side_effects=True),
    )(padded.reshape(members, share, width))
    return result.reshape(share * members, width)[:count]


def local(k_coeffs, v_basis):
    cells_x, cells_y, cells_z, rank = k_coeffs.shape
    slabs = lax.axis_size("slab")
    bricks = lax.axis_size("brick")
    lengths = (cells_x * slabs, cells_y * bricks, cells_z)
    cells = lengths[0] * lengths[1] * lengths[2]
    time_step = CFL / (VMAX * (lengths[0] + lengths[1] + lengths[2]))
    weight_x = 1.0 / cells
    weight_v = (2.0 * VMAX / NVX) ** 3
    nodes = v_basis.shape[0]
    slab, brick = lax.axis_index("slab"), lax.axis_index("brick")
    row_ids = (slab * bricks + brick) * nodes + jnp.arange(nodes, dtype=jnp.int32)
    velocity = velocities(row_ids)
    positive = jnp.maximum(velocity, 0.0)
    negative = jnp.minimum(velocity, 0.0)
    square = jnp.sum(velocity * velocity, axis=0)
    zero = jnp.zeros_like(square)
    ones = jnp.ones_like(square)
    weights = jnp.stack([ones, velocity[0], velocity[1], velocity[2], square, zero, zero, zero])
    partial = jnp.dot(weights, v_basis, precision=PRECISE) * weight_v
    packed = jnp.concatenate([partial, k_coeffs.reshape(-1, rank)], axis=0)
    gathered = gather(packed, 1)
    vectors = jnp.sum(gathered[:, :, :, :8], axis=(0, 1, 2))
    blocks = gathered[:, :, :, 8:].reshape(2, slabs, bricks // 2, cells_x, cells_y, cells_z, rank)
    grid = blocks.transpose(1, 3, 2, 0, 4, 5, 6).reshape(lengths + (rank,))
    flat = grid.reshape(cells, rank)

    rows = cell_state(vectors, flat)
    velocity_rows = jnp.pad(velocity, ((0, 5), (0, 0)))
    mproj_part = project(rows.T, velocity_rows, v_basis, weight_v)
    sides = jnp.concatenate([positive, negative], axis=0) * weight_v
    transport_part = lax.dot_general(
        sides[:, :, None] * v_basis[None],
        v_basis,
        (((1,), (0,)), ((), ())),
        precision=FAST,
    )
    summed = all_reduce(jnp.concatenate([mproj_part, transport_part.reshape(6 * rank, rank)]), 2)
    mproj = summed[:cells]
    transport = summed[cells:]

    fwd = forward_slopes(grid, lengths)
    back = [jnp.roll(item, 1, axis=d) for d, item in enumerate(fwd)]
    slopes = jnp.concatenate([item.reshape(cells, rank) for item in back + fwd], axis=1)
    flux = jnp.dot(slopes, transport, precision=FAST)
    advanced = flat - time_step * flux + COLLIDE * (mproj - flat)

    new_grid = advanced.reshape(lengths + (rank,))
    sides_new = [item.reshape(cells, rank) for item in forward_slopes(new_grid, lengths)]
    over_cells = (((0,), (0,)), ((), ()))
    gram = lax.dot_general(advanced, advanced, over_cells, precision=PRECISE) * weight_x
    raw = [
        lax.dot_general(advanced, item, over_cells, precision=FAST) * weight_x
        for item in sides_new + [mproj]
    ]
    factor = lax.linalg.cholesky(gram, symmetrize_input=False)
    inverse = inverse_of(factor)
    plus = jnp.einsum("ab,kbc,dc->kad", inverse, jnp.stack(raw[:3]), inverse, precision=PRECISE)
    minus = -plus.transpose(0, 2, 1)
    projected = jnp.dot(inverse, raw[3], precision=PRECISE)
    both = jnp.concatenate([minus, plus], axis=0)
    middle = jnp.einsum("kab,cb->akc", both, factor, precision=PRECISE).reshape(rank, 6 * rank)
    hat = factor.T
    coupling_mid = (
        hat
        + time_step * jnp.dot(middle, transport, precision=PRECISE)
        - COLLIDE * (projected - hat)
    )

    velocity_columns = velocity_rows.T
    back_raw = fold(rows, velocity_columns, advanced, weight_x)
    back_proj = lax.dot_general(back_raw, inverse, (((1,), (1,)), ((), ())), precision=FAST)
    lnow = lax.dot_general(v_basis, coupling_mid, (((1,), (1,)), ((), ())), precision=FAST)
    turned = both.transpose(2, 0, 1).reshape(rank, 6 * rank)
    moved = jnp.dot(lnow, turned, precision=FAST)
    side_columns = jnp.concatenate([positive, negative], axis=0).T
    drift = sum(
        side_columns[:, k : k + 1] * moved[:, k * rank : (k + 1) * rank] for k in range(6)
    )
    lnew = lnow - time_step * drift + COLLIDE * (back_proj - lnow)
    gram_v = lax.dot_general(lnew, lnew, over_cells, precision=PRECISE) * weight_v
    gram_v = small_all_reduce(gram_v, 3)
    coupling = lax.linalg.cholesky(gram_v, symmetrize_input=False)
    inverse_v = inverse_of(coupling)
    basis_v = lax.dot_general(lnew, inverse_v, (((1,), (1,)), ((), ())), precision=FAST)
    own = lax.dynamic_slice(
        new_grid,
        (slab * cells_x, brick * cells_y, 0, 0),
        (cells_x, cells_y, cells_z, rank),
    ).reshape(-1, rank)
    basis_x = lax.dot_general(own, inverse, (((1,), (1,)), ((), ())), precision=FAST)
    return basis_x.reshape(k_coeffs.shape), coupling, basis_v


def solution(mesh):
    return jax.shard_map(
        local,
        mesh=mesh,
        in_specs=(P("slab", "brick", None, None), P(("slab", "brick"), None)),
        out_specs=(P("slab", "brick", None, None), P(), P(("slab", "brick"), None)),
        check_vma=False,
    )
```
